128 devices in a mesh: grp: 2 (over z_lo), fsdp: 16 (over x, z_hi, core), item: 4 (over y).
Axes of the slice: x: 4, y: 4, z: 4 (z_hi: 2, z_lo: 2; z = z_hi * 2 + z_lo), core: 2. Of those that a mesh axis runs over, the one named last changes fastest.
Arguments:
- hidden_states: bfloat16 [8192, 16, 4096], P(('grp', 'fsdp', 'item')), may hold values from -6 to 6
- positives: bfloat16 [8192, 1024], P(('grp', 'fsdp', 'item')), may hold values from -6 to 6
- negatives: int32 [8192, 32], P(('grp', 'fsdp', 'item')), may hold values from 0 to 4095, as said below
- lengths: int32 [8192], P(('grp', 'fsdp', 'item')), may hold values from 1 to 16, as said below
- norm_gain: bfloat16 [4096], replicated, may hold values from 0.25 to 1.75
- proj_weight: bfloat16 [4096, 1024], P('fsdp'), may hold values from -0.09375 to 0.09375
- pool_query: float32 [1024], replicated, may hold values from -6 to 6
- slab: bfloat16 [4096, 1024], P('item'), may hold values from -6 to 6
Outputs:
- grad_proj: float32 [4096, 1024], P('fsdp')
- grad_query: float32 [1024], replicated
- mean_loss: float32 [], replicated
The draws below stay inside these ranges and needn't reach their ends.
Inputs may be any that keep to these rules, and one draw needn't show every extreme that they name: `negatives`: entries 8 o to 8 (o + 1) - 1 of each query's list are rows of owner block o, the slab rows 1024 o to 1024 (o + 1) - 1; a row may repeat. The first lengths[q] token slots of query q are valid.
All inputs are finite; a program needn't handle non-finite values.
Results may differ from the reference program's by a relative error of at most 0.0043.
Values may be sent and summed in bfloat16 or wider, within the bound.
A program may use at most 128 MiB of HBM per device.

```python
import math
import jax
import jax.numpy as jnp
from jax import lax

D = 4096
P_SIZE = 1024
SEQ = 16
NEG_OWN = 8
Q_DEV = 64
SLAB_DEV = 1024
QUERIES = 8192
NEG = 32
SLAB = 4096


def draw_negatives(key, part):
    owners = NEG // NEG_OWN
    picked_rows = jax.random.randint(key, (QUERIES, owners, NEG_OWN), 0, SLAB_DEV)
    owner_base = jnp.arange(owners, dtype=jnp.int32)[None, :, None] * SLAB_DEV
    values = (picked_rows + owner_base).reshape(QUERIES, NEG)
    values = values.at[0, 0].set(0).at[0, NEG - 1].set(SLAB - 1)
    return values.astype(jnp.int32)


def draw_lengths(key, part):
    lengths_drawn = jax.random.randint(key, (QUERIES,), 1, SEQ + 1)
    lengths_drawn = lengths_drawn.at[0].set(SEQ).at[1].set(1)
    return lengths_drawn.astype(jnp.int32)


def level_of(own_key, extent, pieces, smallest, top_value):
    gain = 1.0
    for dim, parts in pieces:
        draws = jax.random.uniform(jax.random.fold_in(jax.random.fold_in(own_key, 6), dim), (parts,), jnp.float32, smallest / len(pieces), top_value / len(pieces))
        gain = gain * jnp.repeat(jnp.exp(draws), extent[dim] // parts).reshape((-1,) + (1,) * (len(extent) - 1 - dim))
    return gain


def normal_values(own_key, extent, spread, reach, shards=(), kind=jnp.bfloat16):
    values = spread * jax.random.normal(own_key, extent, jnp.float32)
    if shards:
        values = values * level_of(own_key, extent, shards, -0.22, 0.18)
    return jnp.clip(values, -reach, reach).astype(kind)


def setup_inputs(seed: int = 0) -> dict:
    streams_of = jax.random.split(jax.random.key(seed), 9)
    hidden_states = normal_values(streams_of[0], (QUERIES, SEQ, D), 1.0, 6.0, ((0, 128),))
    positives = normal_values(streams_of[1], (QUERIES, P_SIZE), 1.0, 6.0, ((0, 128),))
    negatives = draw_negatives(jax.random.fold_in(streams_of[8], 71), 0)
    lengths = draw_lengths(jax.random.fold_in(streams_of[8], 71), 0)
    norm_gain = jnp.clip(1.0 + 0.15 * jax.random.normal(streams_of[4], (D,), jnp.float32), 0.25, 1.75).astype(jnp.bfloat16)
    proj_weight = normal_values(streams_of[5], (D, P_SIZE), D ** -0.5, 0.09375, ((0, 16),))
    pool_query = normal_values(streams_of[6], (P_SIZE,), 1.0, 6.0, (), jnp.float32)
    slab = normal_values(streams_of[7], (SLAB, P_SIZE), 1.0, 6.0, ((0, 4),))
    return {"hidden_states": hidden_states, "positives": positives, "negatives": negatives, "lengths": lengths, "norm_gain": norm_gain, "proj_weight": proj_weight, "pool_query": pool_query, "slab": slab}


sharpness_divisor = 0.05
norm_eps = 1e-05
embed_eps = 1e-06

def normalize(states, norm_gain):
    flat_states = states.reshape(-1, states.shape[-1]).astype(jnp.float32)
    inv_rms = lax.rsqrt(lax.optimization_barrier(jnp.mean(flat_states * flat_states, axis=1, keepdims=True)) + norm_eps)
    return (flat_states * inv_rms * norm_gain.astype(jnp.float32)).astype(jnp.bfloat16)

def gated_pool(token_proj, lengths, pool_query, seq_len):
    queries = lengths.shape[0]
    proj_width = token_proj.shape[1]
    tokens = token_proj.reshape(queries, seq_len, proj_width)
    gate_vals = jax.nn.sigmoid(jnp.einsum('qsp,p->qs', tokens, pool_query, precision=lax.Precision.HIGHEST) / math.sqrt(proj_width))
    position = lax.broadcasted_iota(jnp.int32, (queries, seq_len), 1)
    weight = jnp.where(position < lengths[:, None], 1.0, 0.0).astype(jnp.float32) / lengths[:, None].astype(jnp.float32)
    pooled = jnp.einsum('qs,qsp->qp', weight * gate_vals, tokens, precision=lax.Precision.HIGHEST)
    return (pooled, gate_vals, weight)

def unit_embed(pooled):
    proj_width = pooled.shape[1]
    unit_scale = lax.rsqrt(lax.optimization_barrier(jnp.mean(pooled * pooled, axis=1, keepdims=True)) + embed_eps) / math.sqrt(proj_width)
    return ((pooled * unit_scale).astype(jnp.bfloat16), unit_scale)

def contrast(embedded, positives, neg_rows):
    proj_width = embedded.shape[1]
    encoded_vector_fullprec = embedded.astype(jnp.float32)
    matching_vector_fullprec = positives.astype(jnp.float32)
    sample_vectors_fullprec = neg_rows.astype(jnp.float32)
    matching_multiplier = lax.rsqrt(lax.optimization_barrier(jnp.mean(matching_vector_fullprec * matching_vector_fullprec, axis=1)) + embed_eps) / math.sqrt(proj_width)
    matching_score = jnp.einsum('au,au->a', encoded_vector_fullprec, matching_vector_fullprec, precision=lax.Precision.HIGHEST) * matching_multiplier / sharpness_divisor
    row_sq = jnp.einsum('qnp,qnp->qn', sample_vectors_fullprec, sample_vectors_fullprec, precision=lax.Precision.HIGHEST)
    sample_multiplier = lax.rsqrt(row_sq / proj_width + embed_eps) / math.sqrt(proj_width)
    distractor_score = jnp.einsum('ir,isr->is', encoded_vector_fullprec, sample_vectors_fullprec, precision=lax.Precision.HIGHEST) * sample_multiplier / sharpness_divisor
    logits = jnp.concatenate([matching_score[:, None], distractor_score], axis=1)
    exp_logits = jnp.exp(logits)
    denom_sum = lax.optimization_barrier(jnp.sum(exp_logits, axis=1, keepdims=True))
    prob = exp_logits / denom_sum
    loss_sum = jnp.sum(jnp.log(denom_sum[:, 0]) - matching_score)
    column = lax.broadcasted_iota(jnp.int32, logits.shape, 1)
    score_derivative = prob - jnp.where(column == 0, 1.0, 0.0).astype(jnp.float32)
    matching_contribution = (score_derivative[:, 0] * matching_multiplier / sharpness_divisor)[:, None] * matching_vector_fullprec
    distractor_probability = (score_derivative[:, 1:] * sample_multiplier / sharpness_divisor).astype(jnp.bfloat16)
    grad_embed = matching_contribution + jnp.einsum('qn,qnp->qp', distractor_probability.astype(jnp.float32), sample_vectors_fullprec, precision=lax.Precision.HIGHEST)
    return (loss_sum, grad_embed)

def backward(token_proj, pooled, unit_scale, grad_embed, gate_vals, weight, pool_query, seq_len):
    queries, proj_width = pooled.shape
    tokens = token_proj.reshape(queries, seq_len, proj_width)
    mean_sq = lax.optimization_barrier(jnp.mean(pooled * pooled, axis=1, keepdims=True))
    radial = lax.optimization_barrier(jnp.sum(pooled * grad_embed, axis=1, keepdims=True))
    grad_pooled = unit_scale * grad_embed - pooled * radial * unit_scale / (proj_width * (mean_sq + embed_eps))
    proj_dot = jnp.einsum('qsp,qp->qs', tokens, grad_pooled, precision=lax.Precision.HIGHEST)
    gate_slope = weight * gate_vals * (1.0 - gate_vals) * proj_dot / math.sqrt(proj_width)
    grad_tokens = (weight * gate_vals)[:, :, None] * grad_pooled[:, None, :] + gate_slope[:, :, None] * pool_query[None, None, :]
    grad_query = jnp.einsum('qs,qsp->p', gate_slope, tokens, precision=lax.Precision.HIGHEST)
    return (grad_tokens.reshape(queries * seq_len, proj_width).astype(jnp.bfloat16), grad_query)

def reference(hidden_states, positives, negatives, lengths, norm_gain, proj_weight, pool_query, slab):
    queries, seq_len, model_width = hidden_states.shape
    proj_width = proj_weight.shape[1]
    blocks = queries // Q_DEV

    def one_block(carried, block_data):
        grad_weight, grad_pool_sum, loss_total = carried
        states, block_pos, block_negs, block_lengths = block_data
        normed = normalize(states, norm_gain)
        token_proj = jnp.dot(normed, proj_weight, preferred_element_type=jnp.float32)
        pooled, gate_vals, weight = gated_pool(token_proj, block_lengths, pool_query, seq_len)
        embedded, unit_scale = unit_embed(pooled)
        neg_rows = jnp.take(slab, block_negs, axis=0)
        loss_part, grad_embed = contrast(embedded, block_pos, neg_rows)
        grad_tokens, query_part = backward(token_proj, pooled, unit_scale, grad_embed, gate_vals, weight, pool_query, seq_len)
        grad_weight = grad_weight + lax.dot_general(normed, grad_tokens, (((0,), (0,)), ((), ())), preferred_element_type=jnp.float32)
        return ((grad_weight, grad_pool_sum + query_part, loss_total + loss_part), None)
    initial = (jnp.zeros((model_width, proj_width), jnp.float32), jnp.zeros((proj_width,), jnp.float32), jnp.zeros((), jnp.float32))
    block_inputs = (hidden_states.reshape(blocks, Q_DEV, seq_len, model_width), positives.reshape(blocks, Q_DEV, proj_width), negatives.reshape(blocks, Q_DEV, negatives.shape[1]), lengths.reshape(blocks, Q_DEV))
    (grad_proj, grad_query, loss_total), _ = lax.scan(one_block, initial, block_inputs)
    return (grad_proj, grad_query, loss_total / queries)
```

```python
import functools
import math

import jax
import jax.numpy as jnp
from jax import lax
from jax.experimental import pallas as pl
from jax.experimental.pallas import tpu as pltpu
from jax.sharding import PartitionSpec as P

MESH = pl.DeviceIdType.MESH
BF = jnp.bfloat16
F32 = jnp.float32
TEMP = 0.05
NORM_EPS = 1e-5
EMB_EPS = 1e-6

COLX = (0, 128)
COLY = (128, 256)
COLZ = (384, 128)

N_SEM = 112


def dev(x, y, z, c):
    return (lax.rem(z, 2), x * 4 + (z // 2) * 2 + c, y)


def mo(v, m):
    return pl.multiple_of(v, m)


def split2(v):
    hi = v.astype(BF)
    lo = (v - hi.astype(F32)).astype(BF)
    return hi, lo


def col_to_row(v, n):
    return jnp.transpose(jnp.broadcast_to(v, (n, 128)))[0:1, :]


def kernel(
    h_ref, pos_ref, neg_ref, wt_ref, gain_ref, w_ref, pq_ref, slab_ref,
    out_ref, gq_ref, loss_ref,
    XN, WO, WH, V, SLAB, SCR, NG, CM, LG, AT, NB, ACC, PO, EA, WB, GS, GR, DS, DR,
    GP, NTS, NTR, GA, PA, PBS, PBR, PCS, PCR, PG, OG, UP, UR, SACC, Z, ZR, GQ,
    ss, rs, hs, ls,
):
    g_i = lax.axis_index("grp")
    f_i = lax.axis_index("fsdp")
    y = lax.axis_index("item")
    x = f_i // 4
    zh = lax.rem(f_i // 2, 2)
    c = lax.rem(f_i, 2)
    z = zh * 2 + g_i
    zl = g_i
    zf = 3 - z
    oc = 1 - c

    def xs(d):
        return lax.rem(x + d, 4)

    def ys(d):
        return lax.rem(y + d, 4)

    def zs(d):
        return lax.rem(z + d, 4)

    hcp = []
    for i in range(8):
        cp = pltpu.make_async_copy(
            h_ref.at[pl.ds(i * 128, 128)], XN.at[pl.ds(i * 128, 128)], hs.at[i]
        )
        hcp.append(cp)
    own_w = pltpu.make_async_copy(
        w_ref.at[:, pl.ds(mo(c * 512, 512), 512)], WO.at[c], ls.at[0]
    )
    slab_cp = pltpu.make_async_copy(slab_ref, SLAB, ls.at[1])
    own_w.start()
    hcp[0].start()

    peers = []
    for dx in range(4):
        for fl in range(2):
            for dc in range(2):
                if (dx, fl, dc) != (0, 0, 0):
                    peers.append(dev(xs(dx), y, zf if fl else z, oc if dc else c))
    for d in (1, 2, 3):
        peers.append(dev(x, ys(d), z, c))
    zg = zh * 2 + (1 - zl)
    zo = 3 - zg
    for zz in (zg, zo):
        peers.append(dev(x, y, zz, c))
    for d in (1, 2, 3):
        peers.append(dev(x, ys(d), zg, c))
    bar = pltpu.get_barrier_semaphore()
    for p in peers:
        pl.semaphore_signal(bar, inc=1, device_id=p, device_id_type=MESH)
    pl.semaphore_wait(bar, len(peers))

    started = []

    def send(src, dst, to):
        k = len(started)
        cp = pltpu.make_async_remote_copy(
            src_ref=src, dst_ref=dst, send_sem=ss.at[k], recv_sem=rs.at[k],
            device_id=to, device_id_type=MESH,
        )
        cp.start()
        started.append(cp)
        return cp

    def recv(cps):
        for cp in cps:
            cp.wait_recv()

    sib = dev(x, y, z, oc)
    k_w = send(w_ref.at[:, pl.ds(mo(oc * 512, 512), 512)], WO.at[c], sib)
    for i in range(1, 8):
        hcp[i].start()
    slab_cp.start()
    k_neg = [
        send(neg_ref.at[ys(d)], NG.at[y], dev(x, ys(d), z, c)) for d in (1, 2, 3)
    ]
    NG[y] = neg_ref[y]

    wf = jnp.sum(w_ref[...].astype(F32) * pq_ref[...], axis=1, keepdims=True)
    vcol = mo(f_i * 256, 256)
    V[:, pl.ds(vcol, 256)] = col_to_row(wf, 256)
    k_v = []
    for dx in range(4):
        for fl in range(2):
            for dc in range(2):
                if (dx, fl, dc) != (0, 0, 0):
                    k_v.append(
                        send(
                            V.at[:, pl.ds(vcol, 256)], V.at[:, pl.ds(vcol, 256)],
                            dev(xs(dx), y, zf if fl else z, oc if dc else c),
                        )
                    )

    own_w.wait()
    k_w.wait_recv()
    cx = pl.ds(*COLX)
    cy = pl.ds(*COLY)
    cz = pl.ds(*COLZ)
    wo5 = WO.reshape(2, 2, 4, 32, 512)
    k_xp = send(wo5.at[:, :, :, :, cx], WH.at[x, zh, :, :, :, :, cx], dev(x, y, zf, c))
    k_yp = []
    for dx in range(4):
        for fl in range(2):
            if (dx, fl) != (0, 0):
                k_yp.append(
                    send(
                        wo5.at[:, :, y, :, cy], WH.at[x, zh, :, :, y, :, cy],
                        dev(xs(dx), y, zf if fl else z, c),
                    )
                )
    k_zp = [
        send(
            wo5.at[:, zl, :, :, cz], WH.at[x, zh, :, zl, :, :, cz], dev(xs(d), y, z, c)
        )
        for d in (1, 2, 3)
    ]
    k_xm = [
        send(wo5.at[:, :, :, :, cx], WH.at[x, zh, :, :, :, :, cx], dev(xs(d), y, z, c))
        for d in (1, 2, 3)
    ]
    for ci in range(2):
        for a in range(2):
            WH[x, zh, ci, a, :, :, cx] = wo5[ci, a, :, :, cx]
            WH[x, zh, ci, a, y, :, cy] = wo5[ci, a, y, :, cy]
        WH[x, zh, ci, zl, :, :, cz] = wo5[ci, zl, :, :, cz]

    def norm_rows(i, carry):
        r = pl.ds(mo(i * 16, 16), 16)
        ms = jnp.zeros((16, 128), F32)
        for j in range(8):
            xv = XN[r, j * 512 : (j + 1) * 512].astype(F32)
            sq = xv * xv
            ms = ms + ((sq[:, 0:128] + sq[:, 128:256]) + (sq[:, 256:384] + sq[:, 384:512]))
        inv = lax.rsqrt(jnp.sum(ms, axis=1, keepdims=True) / 4096.0 + NORM_EPS)
        for j in range(8):
            cs = slice(j * 512, (j + 1) * 512)
            XN[r, cs] = (
                XN[r, cs].astype(F32) * inv * gain_ref[:, cs].astype(F32)
            ).astype(BF)
        return carry

    for i in range(2):
        hcp[i].wait()
        lax.fori_loop(i * 8, i * 8 + 8, norm_rows, 0, unroll=2)

    k_xp.wait_recv()
    k_xm2 = [
        send(
            WH.at[x, 1 - zh, :, :, :, :, cx], WH.at[x, 1 - zh, :, :, :, :, cx],
            dev(xs(d), y, z, c),
        )
        for d in (1, 2, 3)
    ]
    recv(k_zp)
    k_zm = [
        send(
            WH.at[:, zh, :, zl, :, :, cz], WH.at[:, zh, :, zl, :, :, cz],
            dev(x, y, zs(d), c),
        )
        for d in (1, 2, 3)
    ]
    recv(k_yp)
    k_ym = [
        send(WH.at[:, :, :, :, y, :, cy], WH.at[:, :, :, :, y, :, cy], dev(x, ys(d), z, c))
        for d in (1, 2, 3)
    ]

    for i in range(2, 8):
        hcp[i].wait()
        lax.fori_loop(i * 8, i * 8 + 8, norm_rows, 0, unroll=2)

    recv(k_v)

    def gate_rows(i, carry):
        r = pl.ds(mo(i * 16, 16), 16)
        acc = jnp.zeros((16, 128), F32)
        for j in range(8):
            cs = slice(j * 512, (j + 1) * 512)
            p = XN[r, cs].astype(F32) * V[:, cs]
            acc = acc + ((p[:, 0:128] + p[:, 128:256]) + (p[:, 256:384] + p[:, 384:512]))
        LG[r, :] = jnp.broadcast_to(jnp.sum(acc, axis=1, keepdims=True), (16, 128))
        return carry

    lax.fori_loop(0, 64, gate_rows, 0, unroll=2)

    def at_rows(i, carry):
        r = pl.ds(mo(i * 256, 256), 256)
        gate = jax.nn.sigmoid(LG[r, :] * (1.0 / 32.0))
        LG[r, :] = gate
        wg = gate * wt_ref[r, :]
        q = (lax.broadcasted_iota(jnp.int32, (256, 128), 0) + i * 256) // 16
        lane = lax.broadcasted_iota(jnp.int32, (256, 128), 1)
        hi = wg.astype(BF).astype(F32)
        a = jnp.where(lane == q, hi, 0.0) + jnp.where(lane == q + 64, wg - hi, 0.0)
        AT[:, r] = jnp.transpose(a).astype(BF)
        return carry

    lax.fori_loop(0, 4, at_rows, 0)

    qrow = mo(c * 64, 64)

    def n_cols(i, carry):
        cs = pl.ds(mo(i * 512, 512), 512)
        rr = jnp.dot(AT[...], XN[:, cs], preferred_element_type=F32)
        hi, lo = split2(rr[:64] + rr[64:])
        NB[0, pl.ds(qrow, 64), cs] = hi
        NB[1, pl.ds(qrow, 64), cs] = lo
        return carry

    lax.fori_loop(0, 8, n_cols, 0)
    k_n = send(NB.at[:, pl.ds(qrow, 64), :], NB.at[:, pl.ds(qrow, 64), :], sib)

    slab_cp.wait()
    for i in range(4):
        sv = SLAB[i * 256 : (i + 1) * 256, :].astype(F32)
        sm = lax.rsqrt(jnp.sum(sv * sv, axis=1, keepdims=True) / 1024.0 + EMB_EPS)
        SCR[:, i * 256 : (i + 1) * 256] = col_to_row(sm * (1.0 / (32.0 * TEMP)), 256)
    recv(k_neg)

    def count_rows(i, carry):
        src = i // 4
        r = pl.ds(mo(lax.rem(i, 4) * 16, 16), 16)
        ids = NG[src, r, :] - y * 1024
        row = lax.broadcasted_iota(jnp.int32, (16, 1024), 1)
        cnt = jnp.zeros((16, 1024), F32)
        for k in range(8):
            cnt = cnt + jnp.where(row == ids[:, k : k + 1], 1.0, 0.0)
        CM[pl.ds(mo(i * 16, 16), 16), :] = cnt
        return carry

    lax.fori_loop(0, 16, count_rows, 0)

    k_n.wait_recv()

    def nt_block(i, carry):
        xi = i // 2
        zi = lax.rem(i, 2)
        cs = pl.ds(mo(xi * 1024 + zi * 512 + c * 256, 256), 256)
        for p in range(2):
            NTS[xi, p, pl.ds(mo(zi * 256, 256), 256), :] = jnp.transpose(
                NB[p, :, cs].astype(F32)
            ).astype(BF)
        return carry

    lax.fori_loop(0, 8, nt_block, 0)

    recv(k_xm)
    recv(k_xm2)
    recv(k_zm)
    recv(k_ym)
    k_nt = [send(NTS.at[xs(d)], NTR.at[d - 1], dev(xs(d), y, z, c)) for d in (1, 2, 3)]

    ACC[...] = jnp.zeros_like(ACC)

    def pool_k(k, carry):
        w = WH[k // 4, lax.rem(k // 2, 2), lax.rem(k, 2)].reshape(256, 512)
        a = NB[:, :, pl.ds(mo(k * 256, 256), 256)].reshape(256, 256)
        ACC[...] += jnp.dot(a, w, preferred_element_type=F32)
        return carry

    lax.fori_loop(0, 16, pool_k, 0)
    orow = mo(oc * 64, 64)
    PO[c] = ACC[pl.ds(qrow, 64), :] + ACC[pl.ds(128 + qrow, 64), :]
    PO[2 + c] = ACC[pl.ds(orow, 64), :] + ACC[pl.ds(128 + orow, 64), :]
    k_po = send(PO.at[2 + c], PO.at[c], sib)
    k_po.wait_recv()
    pooled = jnp.concatenate([PO[0], PO[1]], axis=1)
    mean_sq = jnp.mean(pooled * pooled, axis=1, keepdims=True)
    unit = lax.rsqrt(mean_sq + EMB_EPS) / 32.0
    emb = (pooled * unit).astype(BF)
    EA[y] = emb
    k_e = [send(EA.at[y], EA.at[y], dev(x, ys(d), z, c)) for d in (1, 2, 3)]

    posf = pos_ref[...].astype(F32)
    pm = lax.rsqrt(jnp.mean(posf * posf, axis=1, keepdims=True) + EMB_EPS) * (
        1.0 / (32.0 * TEMP)
    )
    ps = jnp.sum(emb.astype(F32) * posf, axis=1, keepdims=True) * pm
    pe = jnp.exp(ps)

    recv(k_e)
    ea = EA[...].reshape(256, 1024)
    den = jnp.zeros((256, 1), F32)
    for i in range(4):
        cs = slice(i * 256, (i + 1) * 256)
        s = lax.dot_general(
            ea, SLAB[cs, :], (((1,), (1,)), ((), ())), preferred_element_type=F32
        )
        ew = jnp.exp(s * SCR[:, cs]) * CM[:, cs]
        den = den + jnp.sum(ew, axis=1, keepdims=True)
        WB[:, cs] = (ew * SCR[:, cs]).astype(BF)
    DS[...] = jnp.broadcast_to(den, (256, 128)).reshape(4, 64, 128)
    k_d = [send(DS.at[ys(d)], DR.at[d - 1], dev(x, ys(d), z, c)) for d in (1, 2, 3)]
    for i in range(2):
        cs = slice(i * 512, (i + 1) * 512)
        GS[:, :, cs] = (
            jnp.dot(WB[...], SLAB[:, cs], preferred_element_type=F32)
            .reshape(4, 64, 512)
            .astype(BF)
        )
    k_g = [send(GS.at[ys(d)], GR.at[d - 1], dev(x, ys(d), z, c)) for d in (1, 2, 3)]
    recv(k_d)
    denom = pe + (DS[y] + DR[0] + DR[1] + DR[2])[:, 0:1]
    rden = 1.0 / denom
    loss = jnp.sum(jnp.log(denom) - ps, axis=0, keepdims=True)
    Z[0, :, 4096:4224] = jnp.broadcast_to(loss, (1, 128))
    recv(k_g)
    gsum = (
        GS[y].astype(F32) + GR[0].astype(F32) + GR[1].astype(F32) + GR[2].astype(F32)
    )
    g_emb = (pe * rden - 1.0) * pm * posf + gsum * rden
    radial = jnp.sum(pooled * g_emb, axis=1, keepdims=True)
    g_pool = unit * g_emb - pooled * (radial * unit / (1024.0 * (mean_sq + EMB_EPS)))
    hi, lo = split2(g_pool)
    GP[0, pl.ds(qrow, 64), :] = hi
    GP[1, pl.ds(qrow, 64), :] = lo
    k_gp = send(GP.at[:, pl.ds(qrow, 64), :], GP.at[:, pl.ds(qrow, 64), :], sib)
    k_gp.wait_recv()

    k_ga = [send(GP.at[0], GA.at[d - 1], dev(xs(d), y, z, c)) for d in (1, 2, 3)]

    gph = GP[:, :, pl.ds(mo(c * 512, 512), 512)].reshape(256, 512)

    def u_block(k, carry):
        w = WH[k // 4, lax.rem(k // 2, 2), lax.rem(k, 2)].reshape(256, 512)
        u = lax.dot_general(gph, w, (((1,), (1,)), ((), ())), preferred_element_type=F32)
        UP[:, pl.ds(mo(k * 256, 256), 256)] = u[:128] + u[128:]
        return carry

    lax.fori_loop(0, 16, u_block, 0)
    k_u = send(UP.at[pl.ds(orow, 64), :], UR, sib)

    recv(k_nt)
    PA[...] = jnp.dot(NTS[x, 0], GP[0], preferred_element_type=F32) + jnp.dot(
        NTS[x, 1], GP[0], preferred_element_type=F32
    )
    recv(k_ga)

    def fac(i, carry):
        PA[...] += jnp.dot(NTR[i, 0], GA[i], preferred_element_type=F32) + jnp.dot(
            NTR[i, 1], GA[i], preferred_element_type=F32
        )
        return carry

    lax.fori_loop(0, 3, fac, 0)
    PBS[...] = PA[...].astype(BF).reshape(4, 128, 1024)
    k_pb = [send(PBS.at[zs(d)], PBR.at[d - 1], dev(x, y, zs(d), c)) for d in (1, 2, 3)]

    k_u.wait_recv()
    SACC[...] = jnp.zeros_like(SACC)

    def slope_rows(i, carry):
        r = pl.ds(mo(i * 16, 16), 16)
        uo = pl.ds(qrow + i, 1)
        acc = jnp.zeros((16, 128), F32)
        for j in range(8):
            cs = slice(j * 512, (j + 1) * 512)
            u = UP[uo, cs] + UR[pl.ds(i, 1), cs]
            p = XN[r, cs].astype(F32) * u
            acc = acc + ((p[:, 0:128] + p[:, 128:256]) + (p[:, 256:384] + p[:, 384:512]))
        pd = jnp.sum(acc, axis=1, keepdims=True)
        gate = LG[r, 0:1]
        slope = wt_ref[r, :] * gate * (1.0 - gate) * pd * (1.0 / 32.0)
        for j in range(8):
            cs = slice(j * 512, (j + 1) * 512)
            SACC[:, cs] += XN[r, cs].astype(F32) * slope
        return carry

    lax.fori_loop(0, 64, slope_rows, 0, unroll=2)
    Z[0, :, 0:4096] = jnp.sum(SACC[...], axis=0, keepdims=True)
    ZR[0, c] = Z[0]
    k_z0 = send(Z.at[0], ZR.at[0, c], sib)

    recv(k_pb)
    zrow = mo(z * 128, 128)
    pc = PA[pl.ds(zrow, 128), :] + (
        PBR[0].astype(F32) + PBR[1].astype(F32) + PBR[2].astype(F32)
    )
    PA[0:128, :] = pc
    PCS[...] = pc.astype(BF).reshape(4, 32, 1024)
    k_pc = [send(PCS.at[ys(d)], PCR.at[d - 1], dev(x, ys(d), z, c)) for d in (1, 2, 3)]

    k_z0.wait_recv()
    Z[1] = ZR[0, 0] + ZR[0, 1]
    ZR[1, x] = Z[1]
    k_z1 = [send(Z.at[1], ZR.at[1, x], dev(xs(d), y, z, c)) for d in (1, 2, 3)]

    recv(k_pc)
    piece = PA[pl.ds(mo(y * 32, 32), 32), :] + (
        PCR[0].astype(F32) + PCR[1].astype(F32) + PCR[2].astype(F32)
    )
    PG[...] = piece.astype(BF)
    OG[zl, y] = PG[...]
    k_og = [send(PG, OG.at[zl, y], dev(x, ys(d), z, c)) for d in (1, 2, 3)]
    k_og += [send(PG, OG.at[zl, y], dev(x, ys(d), zg, c)) for d in range(4)]

    recv(k_z1)
    Z[2] = (ZR[1, 0] + ZR[1, 1]) + (ZR[1, 2] + ZR[1, 3])
    ZR[2, y] = Z[2]
    k_z2 = [send(Z.at[2], ZR.at[2, y], dev(x, ys(d), z, c)) for d in (1, 2, 3)]
    recv(k_z2)
    Z[3] = (ZR[2, 0] + ZR[2, 1]) + (ZR[2, 2] + ZR[2, 3])
    ZR[3, z] = Z[3]
    k_z3 = [send(Z.at[3], ZR.at[3, z], dev(x, y, zs(d), c)) for d in (1, 2, 3)]
    recv(k_z3)
    tot = (ZR[3, 0] + ZR[3, 1]) + (ZR[3, 2] + ZR[3, 3])
    Z[4] = tot
    loss_ref[...] = Z[4, :, 4096:4224] * (1.0 / 8192.0)

    row16 = lax.broadcasted_iota(jnp.int32, (16, 256), 0)
    ACC[0:16, :] = jnp.zeros((16, 512), F32)

    def gq_k(k, carry):
        w = WH[k // 4, lax.rem(k // 2, 2), lax.rem(k, 2)].reshape(256, 512)
        sv = Z[4, :, pl.ds(mo(k * 256, 256), 256)]
        h1 = sv.astype(BF).astype(F32)
        r1 = sv - h1
        h2 = r1.astype(BF).astype(F32)
        a = jnp.where(row16 == 0, h1, jnp.where(row16 == 1, h2, jnp.where(row16 == 2, r1 - h2, 0.0)))
        ACC[0:16, :] += jnp.dot(a.astype(BF), w, preferred_element_type=F32)
        return carry

    lax.fori_loop(0, 16, gq_k, 0)
    GQ[c] = jnp.sum(ACC[0:16, :], axis=0, keepdims=True)
    k_gq = send(GQ.at[c], GQ.at[c], sib)

    s_blk = Z[4, :, pl.ds(vcol, 256)]
    s_col = jnp.transpose(jnp.broadcast_to(s_blk, (128, 256)))[:, 0:1]
    recv(k_og)
    og = OG[...].reshape(256, 1024).astype(F32)
    out_ref[...] = og + s_col * pq_ref[...]
    k_gq.wait_recv()
    gq_ref[:, 0:512] = GQ[0]
    gq_ref[:, 512:1024] = GQ[1]

    for cp in started:
        cp.wait_send()


def body(hidden_states, positives, negatives, lengths, norm_gain, proj_weight, pool_query, slab):
    lists = jnp.transpose(negatives.reshape(64, 4, 8), (1, 0, 2))
    lists = jnp.pad(lists, ((0, 0), (0, 0), (0, 120)), constant_values=-1)
    slot = lax.broadcasted_iota(jnp.int32, (64, 16), 1)
    wt = jnp.where(slot < lengths[:, None], 1.0, 0.0).astype(F32) / lengths[:, None].astype(F32)
    vm = pl.BlockSpec(memory_space=pltpu.VMEM)
    anyspace = pl.BlockSpec(memory_space=pl.ANY)
    scratch = [
        pltpu.VMEM((1024, 4096), BF),
        pltpu.VMEM((2, 256, 512), BF),
        pltpu.VMEM((4, 2, 2, 2, 4, 32, 512), BF),
        pltpu.VMEM((1, 4096), F32),
        pltpu.VMEM((1024, 1024), BF),
        pltpu.VMEM((1, 1024), F32),
        pltpu.VMEM((4, 64, 128), jnp.int32),
        pltpu.VMEM((256, 1024), F32),
        pltpu.VMEM((1024, 128), F32),
        pltpu.VMEM((128, 1024), BF),
        pltpu.VMEM((2, 128, 4096), BF),
        pltpu.VMEM((256, 512), F32),
        pltpu.VMEM((4, 64, 512), F32),
        pltpu.VMEM((4, 64, 1024), BF),
        pltpu.VMEM((256, 1024), BF),
        pltpu.VMEM((4, 64, 1024), BF),
        pltpu.VMEM((3, 64, 1024), BF),
        pltpu.VMEM((4, 64, 128), F32),
        pltpu.VMEM((3, 64, 128), F32),
        pltpu.VMEM((2, 128, 1024), BF),
        pltpu.VMEM((4, 2, 512, 128), BF),
        pltpu.VMEM((3, 2, 512, 128), BF),
        pltpu.VMEM((3, 128, 1024), BF),
        pltpu.VMEM((512, 1024), F32),
        pltpu.VMEM((4, 128, 1024), BF),
        pltpu.VMEM((3, 128, 1024), BF),
        pltpu.VMEM((4, 32, 1024), BF),
        pltpu.VMEM((3, 32, 1024), BF),
        pltpu.VMEM((32, 1024), BF),
        pltpu.VMEM((2, 4, 32, 1024), BF),
        pltpu.VMEM((128, 4096), F32),
        pltpu.VMEM((64, 4096), F32),
        pltpu.VMEM((16, 4096), F32),
        pltpu.VMEM((5, 1, 4224), F32),
        pltpu.VMEM((4, 4, 1, 4224), F32),
        pltpu.VMEM((2, 1, 512), F32),
        pltpu.SemaphoreType.DMA((N_SEM,)),
        pltpu.SemaphoreType.DMA((N_SEM,)),
        pltpu.SemaphoreType.DMA((8,)),
        pltpu.SemaphoreType.DMA((2,)),
    ]
    grad, gq, loss = pl.pallas_call(
        kernel,
        out_shape=(
            jax.ShapeDtypeStruct((256, 1024), F32),
            jax.ShapeDtypeStruct((1, 1024), F32),
            jax.ShapeDtypeStruct((1, 128), F32),
        ),
        in_specs=[anyspace, vm, vm, vm, vm, vm, vm, anyspace],
        out_specs=(vm, vm, vm),
        scratch_shapes=scratch,
        compiler_params=pltpu.CompilerParams(
            collective_id=0, has_side_effects=True, vmem_limit_bytes=60 * 2**20
        ),
    )(
        hidden_states.reshape(1024, 4096), positives, lists, wt.reshape(1024, 1),
        norm_gain.reshape(1, 4096), proj_weight, pool_query.reshape(1, 1024), slab,
    )
    return grad, gq.reshape(1024), loss[0, 0]


def solution(mesh):
    return jax.shard_map(
        body,
        mesh=mesh,
        in_specs=(
            P(("grp", "fsdp", "item"), None, None),
            P(("grp", "fsdp", "item"), None),
            P(("grp", "fsdp", "item"), None),
            P(("grp", "fsdp", "item")),
            P(),
            P("fsdp", None),
            P(),
            P("item", None),
        ),
        out_specs=(P("fsdp", None), P(), P()),
        check_vma=False,
    )
```

```python
import functools
import math

import jax
import jax.numpy as jnp
from jax import lax
from jax.experimental import pallas as pl
from jax.experimental.pallas import tpu as pltpu
from jax.sharding import PartitionSpec as P

MESH = pl.DeviceIdType.MESH
BF = jnp.bfloat16
F32 = jnp.float32
TEMP = 0.05
NORM_EPS = 1e-5
EMB_EPS = 1e-6

COLX = (0, 128)
COLY = (128, 256)
COLZ = (384, 128)

N_SEM = 112


def dev(x, y, z, c):
    return (lax.rem(z, 2), x * 4 + (z // 2) * 2 + c, y)


def mo(v, m):
    return pl.multiple_of(v, m)


def split2(v):
    hi = v.astype(BF)
    lo = (v - hi.astype(F32)).astype(BF)
    return hi, lo


def col_to_row(v, n):
    return jnp.transpose(jnp.broadcast_to(v, (n, 128)))[0:1, :]


def kernel(
    h_ref, pos_ref, neg_ref, len_ref, gain_ref, w_ref, pq1_ref, slab_ref,
    out_ref, sblk_ref, zt_ref,
    XN, WO, WH, V, SLAB, SCR, TN, NG, CM, LG, WT, GN, AT, NB, ACC, PO, EA, WB, GS, GR, DS, DR,
    GP, NT, NTX, NTZ, GAX, GAZ, PT, PA, PBS, PBR, PCS, PCR, PG, OG, UP, UR, SACC, Z, ZR, GQ,
    ss, rs, hs, ls,
):
    g_i = lax.axis_index("grp")
    f_i = lax.axis_index("fsdp")
    y = lax.axis_index("item")
    x = f_i // 4
    zh = lax.rem(f_i // 2, 2)
    c = lax.rem(f_i, 2)
    z = zh * 2 + g_i
    zl = g_i
    zf = 3 - z
    oc = 1 - c

    def xs(d):
        return lax.rem(x + d, 4)

    def ys(d):
        return lax.rem(y + d, 4)

    def zs(d):
        return lax.rem(z + d, 4)

    pq = pq1_ref[...].reshape(1, 1024)
    hcp = []
    for i in range(8):
        cp = pltpu.make_async_copy(
            h_ref.at[pl.ds(i * 128, 128)], XN.at[pl.ds(i * 128, 128)], hs.at[i]
        )
        hcp.append(cp)
    own_w = pltpu.make_async_copy(
        w_ref.at[:, pl.ds(mo(c * 512, 512), 512)], WO.at[c], ls.at[0]
    )
    slab_cp = pltpu.make_async_copy(slab_ref, SLAB, ls.at[1])
    own_w.start()
    hcp[0].start()

    peers = []
    for dx in range(4):
        for fl in range(2):
            for dc in range(2):
                if (dx, fl, dc) != (0, 0, 0):
                    peers.append(dev(xs(dx), y, zf if fl else z, oc if dc else c))
    for d in (1, 2, 3):
        peers.append(dev(x, ys(d), z, c))
    zg = zh * 2 + (1 - zl)
    zo = 3 - zg
    for zz in (zg, zo):
        peers.append(dev(x, y, zz, c))
    for d in (1, 2, 3):
        peers.append(dev(x, ys(d), zg, c))
    bar = pltpu.get_barrier_semaphore()
    for p in peers:
        pl.semaphore_signal(bar, inc=1, device_id=p, device_id_type=MESH)
    pl.semaphore_wait(bar, len(peers))

    started = []

    def send(src, dst, to):
        k = len(started)
        cp = pltpu.make_async_remote_copy(
            src_ref=src, dst_ref=dst, send_sem=ss.at[k], recv_sem=rs.at[k],
            device_id=to, device_id_type=MESH,
        )
        cp.start()
        started.append(cp)
        return cp

    def recv(cps):
        for cp in cps:
            cp.wait_recv()

    sib = dev(x, y, z, oc)
    k_w = send(w_ref.at[:, pl.ds(mo(oc * 512, 512), 512)], WO.at[c], sib)
    for i in range(1, 8):
        hcp[i].start()
    slab_cp.start()
    TN[...] = jnp.zeros_like(TN)
    TN[0:32, 0:64] = neg_ref[...]
    NG[y] = jnp.transpose(TN[...])[0:64, :]
    k_neg = [
        send(NG.at[y], NG.at[y], dev(x, ys(d), z, c)) for d in (1, 2, 3)
    ]
    GN[...] = gain_ref[...].astype(F32).reshape(1, 4096)

    wf = jnp.sum(w_ref[...].astype(F32) * pq, axis=1, keepdims=True)
    vcol = mo(f_i * 256, 256)
    V[:, pl.ds(vcol, 256)] = col_to_row(wf, 256)
    k_v = []
    for dx in range(4):
        for fl in range(2):
            for dc in range(2):
                if (dx, fl, dc) != (0, 0, 0):
                    k_v.append(
                        send(
                            V.at[:, pl.ds(vcol, 256)], V.at[:, pl.ds(vcol, 256)],
                            dev(xs(dx), y, zf if fl else z, oc if dc else c),
                        )
                    )

    own_w.wait()
    k_w.wait_recv()
    cx = pl.ds(*COLX)
    cy = pl.ds(*COLY)
    cz = pl.ds(*COLZ)
    wo5 = WO.reshape(2, 2, 4, 32, 512)
    def xnb(d):
        return dev(xs(d), y, z, c)

    def ynb(d):
        return dev(x, ys(d), z, c)

    def znb(d):
        return dev(x, y, zs(d), c)

    k_xp = send(wo5.at[:, :, :, :, cx], WH.at[x, zh, :, :, :, :, cx], dev(x, y, zf, c))
    k_yp = {}
    for dx, fl in ((0, 1), (1, 0), (3, 0), (1, 1), (3, 1), (2, 0), (2, 1)):
        k_yp[dx, fl] = send(
            wo5.at[:, :, y, :, cy], WH.at[x, zh, :, :, y, :, cy],
            dev(xs(dx), y, zf if fl else z, c),
        )
    k_zp = [
        send(wo5.at[:, zl, :, :, cz], WH.at[x, zh, :, zl, :, :, cz], xnb(d))
        for d in (1, 3, 2)
    ]
    k_xm = [
        send(wo5.at[:, :, :, :, cx], WH.at[x, zh, :, :, :, :, cx], xnb(d))
        for d in (1, 3)
    ]
    for ci in range(2):
        for a in range(2):
            WH[x, zh, ci, a, :, :, 0:384] = wo5[ci, a, :, :, 0:384]
        WH[x, zh, ci, zl, :, :, cz] = wo5[ci, zl, :, :, cz]

    near = []
    far = []

    def step_x2():
        k_xp.wait_recv()
        r = WH.at[x, 1 - zh, :, :, :, :, cx]
        return [send(r, r, xnb(d)) for d in (1, 3)]

    def step_y(dx):
        for fl in range(2):
            if (dx, fl) != (0, 0):
                k_yp[dx, fl].wait_recv()
        xg = xs(4 - dx)
        r = WH.at[x, 1 - zh, :, :, y, :, cy] if dx == 0 else WH.at[xg, :, :, :, y, :, cy]
        return [send(r, r, ynb(d)) for d in (1, 3)]

    def step_z():
        recv(k_zp)
        r = WH.at[:, zh, :, zl, :, :, cz]
        return [send(r, r, znb(d)) for d in (1, 3)]

    def relay(cps, reg, nb, rest):
        cps[0].wait_recv()
        r = reg(3, 0)
        rest.append(send(r, r, nb(1)))
        cps[1].wait_recv()
        r = reg(1, 1)
        rest.append(send(r, r, nb(3)))

    def relay_x(cps, zz):
        relay(cps, lambda d, h: WH.at[xs(d), zz, h, :, :, :, cx], xnb, far)

    def relay_y(cps, dx):
        if dx == 0:
            relay(cps, lambda d, h: WH.at[x, 1 - zh, h, :, ys(d), :, cy], ynb, near)
        else:
            relay(cps, lambda d, h: WH.at[xs(4 - dx), :, h, :, ys(d), :, cy], ynb, far if dx == 2 else near)

    def relay_z(cps):
        def reg(d, h):
            zz = zs(d)
            return WH.at[:, zz // 2, h, lax.rem(zz, 2), :, :, cz]

        relay(cps, reg, znb, near)

    def norm_rows(i, carry):
        r = pl.ds(mo(i * 16, 16), 16)
        ms = jnp.zeros((16, 128), F32)
        for j in range(8):
            xv = XN[r, j * 512 : (j + 1) * 512].astype(F32)
            sq = xv * xv
            ms = ms + ((sq[:, 0:128] + sq[:, 128:256]) + (sq[:, 256:384] + sq[:, 384:512]))
        inv = lax.rsqrt(jnp.sum(ms, axis=1, keepdims=True) / 4096.0 + NORM_EPS)
        for j in range(8):
            cs = slice(j * 512, (j + 1) * 512)
            XN[r, cs] = (
                XN[r, cs].astype(F32) * inv * GN[:, cs]
            ).astype(BF)
        return carry

    def norm_chunk(i):
        hcp[i].wait()
        lax.fori_loop(i * 8, i * 8 + 8, norm_rows, 0, unroll=2)

    norm_chunk(0)
    norm_chunk(1)
    k_y0 = step_y(0)
    k_xm2 = step_x2()
    norm_chunk(2)
    norm_chunk(3)
    k_y1 = step_y(1)
    k_y3 = step_y(3)
    norm_chunk(4)
    norm_chunk(5)
    k_y2 = step_y(2)
    k_zm = step_z()
    norm_chunk(6)
    norm_chunk(7)

    recv(k_v)

    def gate_rows(i, carry):
        r = pl.ds(mo(i * 16, 16), 16)
        acc = jnp.zeros((16, 128), F32)
        for j in range(8):
            cs = slice(j * 512, (j + 1) * 512)
            p = XN[r, cs].astype(F32) * V[:, cs]
            acc = acc + ((p[:, 0:128] + p[:, 128:256]) + (p[:, 256:384] + p[:, 384:512]))
        LG[r, :] = jnp.broadcast_to(jnp.sum(acc, axis=1, keepdims=True), (16, 128))
        n = jnp.full((16, 128), len_ref[i], jnp.int32)
        slot = lax.broadcasted_iota(jnp.int32, (16, 128), 0)
        WT[r, :] = jnp.where(slot < n, 1.0, 0.0) / n.astype(F32)
        return carry

    lax.fori_loop(0, 32, gate_rows, 0, unroll=2)
    relay_y(k_y0, 0)
    lax.fori_loop(32, 64, gate_rows, 0, unroll=2)
    relay_y(k_y1, 1)
    relay_x(k_xm, zh)

    def at_rows(i, carry):
        r = pl.ds(mo(i * 256, 256), 256)
        gate = jax.nn.sigmoid(LG[r, :] * (1.0 / 32.0))
        LG[r, :] = gate
        wg = gate * WT[r, :]
        q = (lax.broadcasted_iota(jnp.int32, (256, 128), 0) + i * 256) // 16
        lane = lax.broadcasted_iota(jnp.int32, (256, 128), 1)
        hi = wg.astype(BF).astype(F32)
        a = jnp.where(lane == q, hi, 0.0) + jnp.where(lane == q + 64, wg - hi, 0.0)
        AT[:, r] = jnp.transpose(a).astype(BF)
        return carry

    lax.fori_loop(0, 4, at_rows, 0)

    qrow = mo(c * 64, 64)

    def n_cols(i, carry):
        cs = pl.ds(mo(i * 512, 512), 512)
        rr = jnp.dot(AT[...], XN[:, cs], preferred_element_type=F32)
        hi, lo = split2(rr[:64] + rr[64:])
        NB[0, pl.ds(qrow, 64), cs] = hi
        NB[1, pl.ds(qrow, 64), cs] = lo
        return carry

    lax.fori_loop(0, 4, n_cols, 0)
    relay_y(k_y3, 3)
    relay_x(k_xm2, 1 - zh)
    lax.fori_loop(4, 8, n_cols, 0)
    relay_z(k_zm)
    relay_y(k_y2, 2)
    k_n = send(NB.at[:, pl.ds(qrow, 64), :], NB.at[:, pl.ds(qrow, 64), :], sib)

    slab_cp.wait()
    for i in range(4):
        sv = SLAB[i * 256 : (i + 1) * 256, :].astype(F32)
        sm = lax.rsqrt(jnp.sum(sv * sv, axis=1, keepdims=True) / 1024.0 + EMB_EPS)
        SCR[:, i * 256 : (i + 1) * 256] = col_to_row(sm * (1.0 / (32.0 * TEMP)), 256)
    recv(k_neg)

    def count_rows(i, carry):
        src = i // 4
        r = pl.ds(mo(lax.rem(i, 4) * 16, 16), 16)
        ids = NG[src, r, :] - y * 1024
        row = lax.broadcasted_iota(jnp.int32, (16, 128), 1)
        cnt = [jnp.zeros((16, 128), F32) for _ in range(8)]
        for k in range(8):
            own = [
                jnp.broadcast_to(ids[:, 8 * o + k : 8 * o + k + 1], (16, 128))
                for o in range(4)
            ]
            idb = jnp.where(y < 2, jnp.where(y == 0, own[0], own[1]), jnp.where(y == 2, own[2], own[3]))
            idb = idb - row
            for t in range(8):
                cnt[t] = cnt[t] + jnp.where(idb == t * 128, 1.0, 0.0)
        for t in range(8):
            CM[pl.ds(mo(i * 16, 16), 16), t * 128 : (t + 1) * 128] = cnt[t]
        return carry

    lax.fori_loop(0, 16, count_rows, 0)

    k_n.wait_recv()

    def nt_block(i, carry):
        xi = i // 2
        zi = lax.rem(i, 2)
        cs = pl.ds(mo(xi * 1024 + zi * 512 + c * 256, 256), 256)
        for p in range(2):
            t = jnp.transpose(NB[p, :, cs].astype(F32)).astype(BF)
            NT[xi, 2 * zi, p] = t[0:128]
            NT[xi, 2 * zi + 1, p] = t[128:256]
        return carry

    lax.fori_loop(0, 8, nt_block, 0)

    ACC[...] = jnp.zeros_like(ACC)

    def pool_k(k, carry):
        o = k // 4
        xk = lax.rem(x + o + o // 2 - 2 * (o // 3), 4)
        w = WH[xk, lax.rem(k // 2, 2), lax.rem(k, 2)].reshape(256, 512)
        a = NB[:, :, pl.ds(mo(xk * 1024 + lax.rem(k, 4) * 256, 256), 256)].reshape(256, 256)
        ACC[...] += jnp.dot(a, w, preferred_element_type=F32)
        return carry

    recv(near)
    k_nt = [send(NT.at[xs(d)], NTX.at[d - 1], xnb(d)) for d in (1, 2, 3)]
    k_nt += [send(NT.at[:, zs(d)], NTZ.at[d - 1], znb(d)) for d in (1, 2, 3)]


    lax.fori_loop(0, 12, pool_k, 0)
    recv(far)
    lax.fori_loop(12, 16, pool_k, 0)
    orow = mo(oc * 64, 64)
    PO[c] = ACC[pl.ds(qrow, 64), :] + ACC[pl.ds(128 + qrow, 64), :]
    PO[2 + c] = ACC[pl.ds(orow, 64), :] + ACC[pl.ds(128 + orow, 64), :]
    k_po = send(PO.at[2 + c], PO.at[c], sib)
    k_po.wait_recv()
    pooled = jnp.concatenate([PO[0], PO[1]], axis=1)
    mean_sq = jnp.mean(pooled * pooled, axis=1, keepdims=True)
    unit = lax.rsqrt(mean_sq + EMB_EPS) / 32.0
    emb = (pooled * unit).astype(BF)
    EA[y] = emb
    k_e = {d: send(EA.at[y], EA.at[y], ynb(d)) for d in (1, 3, 2)}

    posf = pos_ref[...].astype(F32)
    pm = lax.rsqrt(jnp.mean(posf * posf, axis=1, keepdims=True) + EMB_EPS) * (
        1.0 / (32.0 * TEMP)
    )
    ps = jnp.sum(emb.astype(F32) * posf, axis=1, keepdims=True) * pm
    pe = jnp.exp(ps)

    def score(g):
        y0, y1 = (ys(3), ys(1)) if g == 0 else (ys(2), y)
        ea = jnp.concatenate([EA[y0], EA[y1]], axis=0)
        den = jnp.zeros((128, 1), F32)
        for i in range(4):
            cs = slice(i * 256, (i + 1) * 256)
            s = lax.dot_general(
                ea, SLAB[cs, :], (((1,), (1,)), ((), ())), preferred_element_type=F32
            )
            cnt = jnp.concatenate(
                [CM[pl.ds(mo(y0 * 64, 64), 64), cs], CM[pl.ds(mo(y1 * 64, 64), 64), cs]], axis=0
            )
            ew = jnp.exp(s * SCR[:, cs]) * cnt
            den = den + jnp.sum(ew, axis=1, keepdims=True)
            WB[:, cs] = (ew * SCR[:, cs]).astype(BF)
        den = jnp.broadcast_to(den, (128, 128))
        DS[y0] = den[0:64]
        DS[y1] = den[64:128]
        for i in range(2):
            cs = slice(i * 512, (i + 1) * 512)
            gr = jnp.dot(WB[...], SLAB[:, cs], preferred_element_type=F32).astype(BF)
            GS[y0, :, cs] = gr[0:64]
            GS[y1, :, cs] = gr[64:128]

    k_e[1].wait_recv()
    k_e[3].wait_recv()
    score(0)
    k_g = [send(GS.at[ys(d)], GR.at[d - 1], ynb(d)) for d in (1, 3)]
    k_d = [send(DS.at[ys(d)], DR.at[d - 1], ynb(d)) for d in (1, 3)]
    k_e[2].wait_recv()
    score(1)
    k_g.append(send(GS.at[ys(2)], GR.at[1], ynb(2)))
    k_d.append(send(DS.at[ys(2)], DR.at[1], ynb(2)))
    recv(k_d)
    denom = pe + (DS[y] + DR[0] + DR[1] + DR[2])[:, 0:1]
    rden = 1.0 / denom
    loss = jnp.sum(jnp.log(denom) - ps, axis=0, keepdims=True)
    Z[0, :, 4096:4224] = jnp.broadcast_to(loss, (1, 128))
    recv(k_g)
    gsum = (
        GS[y].astype(F32) + GR[0].astype(F32) + GR[1].astype(F32) + GR[2].astype(F32)
    )
    g_emb = (pe * rden - 1.0) * pm * posf + gsum * rden
    radial = jnp.sum(pooled * g_emb, axis=1, keepdims=True)
    g_pool = unit * g_emb - pooled * (radial * unit / (1024.0 * (mean_sq + EMB_EPS)))
    hi, lo = split2(g_pool)
    GP[0, pl.ds(qrow, 64), :] = hi
    GP[1, pl.ds(qrow, 64), :] = lo
    k_gp = send(GP.at[:, pl.ds(qrow, 64), :], GP.at[:, pl.ds(qrow, 64), :], sib)
    k_gp.wait_recv()

    k_gx = [send(GP.at[0, :, 0:512], GAX.at[d - 1], xnb(d)) for d in (1, 3, 2)]
    k_gz = [send(GP.at[0, :, 512:1024], GAZ.at[d - 1], znb(d)) for d in (1, 3, 2)]

    gph = GP[:, :, pl.ds(mo(c * 512, 512), 512)].reshape(256, 512)

    def u_block(k, carry):
        w = WH[k // 4, lax.rem(k // 2, 2), lax.rem(k, 2)].reshape(256, 512)
        u = lax.dot_general(gph, w, (((1,), (1,)), ((), ())), preferred_element_type=F32)
        UP[:, pl.ds(mo(k * 256, 256), 256)] = u[:128] + u[128:]
        return carry

    lax.fori_loop(0, 16, u_block, 0)
    k_u = send(UP.at[pl.ds(orow, 64), :], UR, sib)

    recv(k_nt)

    def fac_pair(n0, n1, g0, g1):
        out = None
        gg = jnp.concatenate([g0, g1], axis=0)
        for p in range(2):
            nn = jnp.concatenate([n0(p).reshape(512, 128), n1(p).reshape(512, 128)], axis=1)
            r = jnp.dot(nn, gg, preferred_element_type=F32)
            out = r if out is None else out + r
        return out

    recv(k_gx)
    PT[...] = fac_pair(lambda p: NT[x, :, p], lambda p: NTX[0, :, p], GP[0, :, 0:512], GAX[0])
    PT[...] += fac_pair(lambda p: NTX[1, :, p], lambda p: NTX[2, :, p], GAX[1], GAX[2])
    PBS[0] = PT[...].astype(BF).reshape(4, 128, 512)
    PA[:, 0:512] = PT[pl.ds(mo(z * 128, 128), 128), :]
    k_pb = [send(PBS.at[0, zs(d)], PBR.at[0, d - 1], znb(d)) for d in (1, 3, 2)]
    recv(k_gz)
    PT[...] = fac_pair(lambda p: NT[:, z, p], lambda p: NTZ[0, :, p], GP[0, :, 512:1024], GAZ[0])
    PT[...] += fac_pair(lambda p: NTZ[1, :, p], lambda p: NTZ[2, :, p], GAZ[1], GAZ[2])
    PBS[1] = PT[...].astype(BF).reshape(4, 128, 512)
    PA[:, 512:1024] = PT[pl.ds(mo(x * 128, 128), 128), :]
    k_pb += [send(PBS.at[1, xs(d)], PBR.at[1, d - 1], xnb(d)) for d in (1, 3, 2)]

    k_u.wait_recv()
    SACC[...] = jnp.zeros_like(SACC)

    def slope_rows(i, carry):
        r = pl.ds(mo(i * 16, 16), 16)
        uo = pl.ds(qrow + i, 1)
        acc = jnp.zeros((16, 128), F32)
        for j in range(8):
            cs = slice(j * 512, (j + 1) * 512)
            u = UP[uo, cs] + UR[pl.ds(i, 1), cs]
            p = XN[r, cs].astype(F32) * u
            acc = acc + ((p[:, 0:128] + p[:, 128:256]) + (p[:, 256:384] + p[:, 384:512]))
        pd = jnp.sum(acc, axis=1, keepdims=True)
        gate = LG[r, 0:1]
        slope = WT[r, 0:1] * gate * (1.0 - gate) * pd
        for j in range(8):
            cs = slice(j * 512, (j + 1) * 512)
            SACC[:, cs] += XN[r, cs].astype(F32) * slope
        return carry

    lax.fori_loop(0, 64, slope_rows, 0, unroll=2)
    Z[0, :, 4224:5248] = jnp.zeros((1, 1024), F32)
    Z[0, :, 0:4096] = jnp.sum(SACC[...], axis=0, keepdims=True)
    ZR[0, c] = Z[0]
    k_z0 = send(Z.at[0], ZR.at[0, c], sib)

    recv(k_pb)
    for k in range(2):
        cs = slice(k * 512, (k + 1) * 512)
        PA[:, cs] += (
            PBR[k, 0].astype(F32) + PBR[k, 1].astype(F32) + PBR[k, 2].astype(F32)
        )
    PCS[...] = PA[...].astype(BF).reshape(4, 32, 1024)
    k_pc = [send(PCS.at[ys(d)], PCR.at[d - 1], ynb(d)) for d in (1, 3, 2)]

    k_z0.wait_recv()
    Z[1] = ZR[0, 0] + ZR[0, 1]
    ZR[1, x] = Z[1]
    k_z1 = [send(Z.at[1, :, 0:4224], ZR.at[1, x, :, 0:4224], xnb(d)) for d in (1, 3, 2)]
    recv(k_z1)
    sx = slice(0, 4224)
    Z[2, :, sx] = (ZR[1, 0, :, sx] + ZR[1, 1, :, sx]) + (ZR[1, 2, :, sx] + ZR[1, 3, :, sx])

    row16 = lax.broadcasted_iota(jnp.int32, (16, 256), 0)
    ACC[0:16, :] = jnp.zeros((16, 512), F32)

    def gq_k(k, carry):
        w = WH[k // 4, lax.rem(k // 2, 2), lax.rem(k, 2)].reshape(256, 512)
        sv = Z[2, :, pl.ds(mo(k * 256, 256), 256)]
        h1 = sv.astype(BF).astype(F32)
        r1 = sv - h1
        h2 = r1.astype(BF).astype(F32)
        a = jnp.where(row16 == 0, h1, jnp.where(row16 == 1, h2, jnp.where(row16 == 2, r1 - h2, 0.0)))
        ACC[0:16, :] += jnp.dot(a.astype(BF), w, preferred_element_type=F32)
        return carry

    lax.fori_loop(0, 16, gq_k, 0)
    GQ[c] = jnp.sum(ACC[0:16, :], axis=0, keepdims=True)
    k_gq = send(GQ.at[c], GQ.at[c], sib)

    recv(k_pc)
    piece = PA[pl.ds(mo(y * 32, 32), 32), :] + (
        PCR[0].astype(F32) + PCR[1].astype(F32) + PCR[2].astype(F32)
    )
    PG[...] = piece.astype(BF)
    OG[zl, y] = PG[...]
    k_og = [send(PG, OG.at[zl, y], dev(x, ys(d), zg, c)) for d in (2, 1, 3, 0)]
    k_og += [send(PG, OG.at[zl, y], ynb(d)) for d in (2, 1, 3)]

    k_gq.wait_recv()
    Z[2, :, 4224:4736] = GQ[0]
    Z[2, :, 4736:5248] = GQ[1]
    ZR[2, y] = Z[2]
    k_z2 = [send(Z.at[2], ZR.at[2, y], ynb(d)) for d in (1, 3, 2)]
    recv(k_z2)
    Z[3] = (ZR[2, 0] + ZR[2, 1]) + (ZR[2, 2] + ZR[2, 3])
    ZR[3, z] = Z[3]
    k_z3 = [send(Z.at[3], ZR.at[3, z], znb(d)) for d in (1, 3, 2)]
    recv(k_z3)
    Z[4] = (ZR[3, 0] + ZR[3, 1]) + (ZR[3, 2] + ZR[3, 3])
    sblk_ref[...] = Z[4, :, pl.ds(vcol, 256)]
    zt_ref[...] = Z[4, :, 4096:5248]
    recv(k_og)
    out_ref[...] = OG[...].reshape(256, 1024)

    for cp in started:
        cp.wait_send()


def finish(og_ref, s_ref, z_ref, pq_ref, out_ref, gq_ref, loss_ref):
    col = jnp.transpose(jnp.broadcast_to(s_ref[...] * (1.0 / 32.0), (128, 256)))[:, 0:1]
    out_ref[...] = og_ref[...].astype(F32) + col * pq_ref[...].reshape(1, 1024)
    gq_ref[...] = (z_ref[:, 128:1152] * (1.0 / 32.0)).reshape(1024)
    loss_ref[...] = z_ref[:, 0:128] * (1.0 / 8192.0)


def body(hidden_states, positives, negatives, lengths, norm_gain, proj_weight, pool_query, slab):
    vm = pl.BlockSpec(memory_space=pltpu.VMEM)
    anyspace = pl.BlockSpec(memory_space=pl.ANY)
    scratch = [
        pltpu.VMEM((1024, 4096), BF),
        pltpu.VMEM((2, 256, 512), BF),
        pltpu.VMEM((4, 2, 2, 2, 4, 32, 512), BF),
        pltpu.VMEM((1, 4096), F32),
        pltpu.VMEM((1024, 1024), BF),
        pltpu.VMEM((1, 1024), F32),
        pltpu.VMEM((128, 128), jnp.int32),
        pltpu.VMEM((4, 64, 128), jnp.int32),
        pltpu.VMEM((256, 1024), F32),
        pltpu.VMEM((1024, 128), F32),
        pltpu.VMEM((1024, 128), F32),
        pltpu.VMEM((1, 4096), F32),
        pltpu.VMEM((128, 1024), BF),
        pltpu.VMEM((2, 128, 4096), BF),
        pltpu.VMEM((256, 512), F32),
        pltpu.VMEM((4, 64, 512), F32),
        pltpu.VMEM((4, 64, 1024), BF),
        pltpu.VMEM((128, 1024), BF),
        pltpu.VMEM((4, 64, 1024), BF),
        pltpu.VMEM((3, 64, 1024), BF),
        pltpu.VMEM((4, 64, 128), F32),
        pltpu.VMEM((3, 64, 128), F32),
        pltpu.VMEM((2, 128, 1024), BF),
        pltpu.VMEM((4, 4, 2, 128, 128), BF),
        pltpu.VMEM((3, 4, 2, 128, 128), BF),
        pltpu.VMEM((3, 4, 2, 128, 128), BF),
        pltpu.VMEM((3, 128, 512), BF),
        pltpu.VMEM((3, 128, 512), BF),
        pltpu.VMEM((512, 512), F32),
        pltpu.VMEM((128, 1024), F32),
        pltpu.VMEM((2, 4, 128, 512), BF),
        pltpu.VMEM((2, 3, 128, 512), BF),
        pltpu.VMEM((4, 32, 1024), BF),
        pltpu.VMEM((3, 32, 1024), BF),
        pltpu.VMEM((32, 1024), BF),
        pltpu.VMEM((2, 4, 32, 1024), BF),
        pltpu.VMEM((128, 4096), F32),
        pltpu.VMEM((64, 4096), F32),
        pltpu.VMEM((16, 4096), F32),
        pltpu.VMEM((5, 1, 5248), F32),
        pltpu.VMEM((4, 4, 1, 5248), F32),
        pltpu.VMEM((2, 1, 512), F32),
        pltpu.SemaphoreType.DMA((N_SEM,)),
        pltpu.SemaphoreType.DMA((N_SEM,)),
        pltpu.SemaphoreType.DMA((8,)),
        pltpu.SemaphoreType.DMA((2,)),
    ]
    og, sblk, zt = pl.pallas_call(
        kernel,
        out_shape=(
            jax.ShapeDtypeStruct((256, 1024), BF),
            jax.ShapeDtypeStruct((1, 256), F32),
            jax.ShapeDtypeStruct((1, 1152), F32),
        ),
        in_specs=[anyspace, vm, vm, pl.BlockSpec(memory_space=pltpu.SMEM), vm, vm, vm, anyspace],
        out_specs=(vm, vm, vm),
        scratch_shapes=scratch,
        compiler_params=pltpu.CompilerParams(
            collective_id=0, has_side_effects=True, vmem_limit_bytes=60 * 2**20
        ),
    )(
        hidden_states.reshape(1024, 4096), positives, jnp.transpose(negatives), lengths,
        norm_gain, proj_weight, pool_query, slab,
    )
    grad, gq, loss = pl.pallas_call(
        finish,
        out_shape=(
            jax.ShapeDtypeStruct((256, 1024), F32),
            jax.ShapeDtypeStruct((1024,), F32),
            jax.ShapeDtypeStruct((1, 128), F32),
        ),
        in_specs=[vm, vm, vm, vm],
        out_specs=(vm, vm, vm),
    )(og, sblk, zt, pool_query)
    return grad, gq, loss[0, 0]


def solution(mesh):
    return jax.shard_map(
        body,
        mesh=mesh,
        in_specs=(
            P(("grp", "fsdp", "item"), None, None),
            P(("grp", "fsdp", "item"), None),
            P(("grp", "fsdp", "item"), None),
            P(("grp", "fsdp", "item")),
            P(),
            P("fsdp", None),
            P(),
            P("item", None),
        ),
        out_specs=(P("fsdp", None), P(), P()),
        check_vma=False,
    )
```
